32 devices in a mesh: tm: 2 (over x), row: 4 (over y, core), col: 4 (over z).
Axes of the slice: x: 2, y: 2, z: 4, core: 2. Of those that a mesh axis runs over, the one named last changes fastest.
Arguments:
- returns: bfloat16 [1440, 4096], P('tm', ('row', 'col')), may hold values from -50 to 50
- block_bars: int32 [8], replicated, may hold values from 90 to 180
Outputs:
- correlation: bfloat16 [8, 4096, 4096], P('tm', 'row', 'col')
The draws below stay inside these ranges and needn't reach their ends.
All inputs are finite; a program needn't handle non-finite values.
Results may differ from the reference program's by a relative error of at most 0.0034.
Values may be sent and summed in bfloat16 or wider, within the bound.
A program may use at most 128 MiB of HBM per device.

```python
import jax
import jax.numpy as jnp
from jax import lax

S = 4096
BLK = 180
NBLK = 8


def draw_returns(key, part):
    keys = jax.random.split(jax.random.fold_in(key, 7), 4)
    nrows = NBLK * BLK
    scales = jnp.exp(jax.random.uniform(keys[0], (1, S), jnp.float32, 0.0, jnp.log(10.0)))
    betas = jax.random.uniform(keys[1], (1, S), jnp.float32, -1.0, 1.0)
    factor = jax.random.normal(keys[2], (nrows, 1), jnp.float32)
    noise = jax.random.normal(keys[3], (nrows, S), jnp.float32)
    values = jnp.clip((betas * factor + noise) * scales, -50.0, 50.0)
    return values.astype(jnp.bfloat16)


def touch_ends(values, rng, low, largest):
    extent = values.shape
    index_at = [jax.random.randint(jax.random.fold_in(rng, axis), (), 0, extent[axis]) for axis in range(len(extent))]
    values = values.at[tuple(index_at)].set(low)
    longest = extent.index(max(extent))
    index_at[longest] = (index_at[longest] + 1) % extent[longest]
    return values.at[tuple(index_at)].set(largest)


def setup_inputs(seed: int = 0) -> dict:
    key_list = jax.random.split(jax.random.key(seed), 3)
    return {
        "returns": draw_returns(jax.random.fold_in(key_list[2], 71), 0),
        "block_bars": touch_ends(jax.random.randint(key_list[1], (NBLK,), BLK // 2, BLK + 1), jax.random.fold_in(key_list[1], 1), BLK // 2, BLK).astype(jnp.int32),
    }


def reference(returns, block_bars):
    blocks = returns.reshape(NBLK, BLK, S)

    def advance(carry, item):
        mean_prev, gram_prev, var_prev, count_prev = carry
        rows, count = item
        count_f = count.astype(jnp.float32)
        mask = (jnp.arange(BLK, dtype=jnp.int32)[:, None] < count).astype(jnp.float32)
        values = rows.astype(jnp.float32)
        mean_now = lax.optimization_barrier(jnp.sum(mask * values, axis=0)) / count_f
        centered = (mask * (values - mean_now[None, :])).astype(jnp.bfloat16)
        gram_now = jnp.dot(centered.T, centered, preferred_element_type=jnp.float32)
        cent_f = centered.astype(jnp.float32)
        var_now = lax.optimization_barrier(jnp.sum(cent_f * cent_f, axis=0))
        weight = count_prev * count_f / (count_prev + count_f)
        delta = mean_prev - mean_now
        cov = gram_prev + gram_now + weight * delta[:, None] * delta[None, :]
        var_all = var_prev + var_now + weight * delta * delta
        inverse = lax.rsqrt(var_all)
        corr = (cov * inverse[:, None] * inverse[None, :]).astype(jnp.bfloat16)
        return ((mean_now, gram_now, var_now, count_f), corr)
    start = (jnp.zeros((S,), jnp.float32), jnp.zeros((S, S), jnp.float32), jnp.zeros((S,), jnp.float32), jnp.zeros((), jnp.float32))
    final, output = lax.scan(advance, start, (blocks, block_bars))
    return output
```

```python
import functools

import jax
import jax.numpy as jnp
from jax import lax
from jax.experimental import pallas as pl
from jax.experimental.pallas import tpu as pltpu
from jax.sharding import PartitionSpec as P

TILE = 16
DEPTH = 256
MESH = pl.DeviceIdType.MESH


def up(value, step=TILE):
    return -(-value // step) * step


def down(value, step=TILE):
    return value // step * step


def kernel(
    sizes, nb, blk, bars_ref, x_ref, out_ref,
    raw, lhs, rhs, stats, own_sem, row_send, row_recv, next_send, hub_send, col_recv, relay_send,
):
    T, R, C = sizes
    nbars, width = x_ref.shape
    t, r, c = lax.axis_index("tm"), lax.axis_index("row"), lax.axis_index("col")
    hub = r == c
    last = nb - 1
    cuts = [up(blk * b) for b in range(nb - 1)] + [down(blk * last), nbars]
    spans = [(cuts[b], cuts[b + 1] - cuts[b]) for b in range(nb)]
    spans.append((nbars, nbars - cuts[last]))
    before = nb

    def rows(ch):
        return pl.ds(*spans[ch])

    barrier = pltpu.get_barrier_semaphore()

    def greet(where):
        pl.semaphore_signal(barrier, inc=1, device_id=where, device_id_type=MESH)

    ends = ((c > 0, {"col": c - 1}), (c < C - 1, {"col": c + 1}), (t > 0, {"tm": t - 1}), (t < T - 1, {"tm": t + 1}))
    expected = R - 1
    for there, where in ends:
        pl.when(there)(functools.partial(greet, where))
        expected = expected + there.astype(jnp.int32)
    for step in range(1, R):
        greet({"row": lax.rem(r + step, R)})
    pl.semaphore_wait(barrier, expected)

    def remote(src, dst, send, recv, where):
        return pltpu.make_async_remote_copy(
            src_ref=src, dst_ref=dst, send_sem=send, recv_sem=recv, device_id=where, device_id_type=MESH
        )

    sent = []

    def start(there, make):
        @pl.when(there)
        def _():
            make().start()

        sent.append((there, make))

    def row_copy(ch, k, to_right, src):
        where = {"col": c + 1 if to_right else c - 1}
        return remote(src, raw.at[0, k, rows(ch)], row_send.at[ch, k, int(to_right)], row_recv.at[ch, k], where)

    def own_send(ch):
        src = x_ref.at[rows(ch)]
        start(c < C - 1, lambda: row_copy(ch, c, True, src))
        start(c > 0, lambda: row_copy(ch, c, False, src))

    def spread(there, ch, k, src):
        at_hub = jnp.logical_and(there, hub)
        chips = R // 2
        chip = r // 2
        for step in range(1, chips):
            where = {"row": 2 * lax.rem(chip + step, chips) + lax.rem(k, 2)}
            start(at_hub, lambda where=where, step=step: remote(
                src, raw.at[1, k, rows(ch)], hub_send.at[ch, k, step], col_recv.at[ch, k], where))
        partner = {"row": r + 1 - 2 * lax.rem(r, 2)}
        start(at_hub, lambda: remote(src, raw.at[1, k, rows(ch)], hub_send.at[ch, k, 0], col_recv.at[ch, k], partner))
        if ch == last:
            start(jnp.logical_and(there, t < T - 1), lambda: remote(
                src, raw.at[0, k, rows(before)], next_send.at[k], row_recv.at[before, k], {"tm": t + 1}))

    def row_arrive(there, ch, k):
        @pl.when(there)
        def _():
            piece = raw.at[0, k, rows(ch)]
            remote(piece, piece, next_send.at[k], row_recv.at[ch, k], {"row": r}).wait_recv()

    def row_phase(ch):
        for d in range(1, C):
            for from_left in (True, False):
                k0 = c - d if from_left else c + d
                there = k0 >= 0 if from_left else k0 < C
                k = jnp.clip(k0, 0, C - 1)
                row_arrive(there, ch, k)
                src = raw.at[0, k, rows(ch)]
                on = c < C - 1 if from_left else c > 0
                start(jnp.logical_and(there, on), lambda k=k, src=src, right=from_left: row_copy(ch, k, right, src))
                spread(there, ch, k, src)

    def before_phase():
        for k in range(C):
            row_arrive(t > 0, before, k)
            spread(t > 0, before, jnp.int32(k), raw.at[0, k, rows(before)])

    def col_phase(ch, there):
        relay = jnp.logical_and(there, r // 2 != c // 2)
        partner = {"row": r + 1 - 2 * lax.rem(r, 2)}
        for k in range(C):
            piece = raw.at[1, k, rows(ch)]

            @pl.when(jnp.logical_and(there, jnp.logical_not(hub)))
            def _():
                remote(piece, piece, next_send.at[k], col_recv.at[ch, k], {"row": r}).wait_recv()

            start(jnp.logical_and(relay, lax.rem(r, 2) == k % 2), lambda piece=piece, k=k: remote(
                piece, piece, relay_send.at[ch, k], col_recv.at[ch, k], partner))

    base = t * nb

    def count(j):
        if j:
            return bars_ref[base + j - 1]
        return jnp.where(t > 0, bars_ref[jnp.maximum(base - 1, 0)], 0)

    def center(j):
        b = j - 1 if j else last
        low = down(blk * b)
        depth = up(blk * (b + 1)) - low
        offset = blk * b - low
        first = low if j else spans[before][0]
        n = count(j)
        bar = lax.broadcasted_iota(jnp.int32, (depth, width), 0) - offset
        mask = jnp.logical_and(bar >= 0, bar < n)
        divisor = jnp.full((1, width), jnp.maximum(n, 1).astype(jnp.float32))
        for side in range(2):
            source = 0 if side == 0 else jnp.where(hub, 0, 1)

            def piece(k, carry):
                values = raw[source, k, pl.ds(first, depth), :].astype(jnp.float32)
                mean = jnp.sum(jnp.where(mask, values, 0.0), axis=0, keepdims=True) / divisor
                cent = jnp.where(mask, values - mean, 0.0).astype(jnp.bfloat16)
                wide = cent.astype(jnp.float32)
                stats[side, k, 2 * j : 2 * j + 1, :] = mean
                stats[side, k, 2 * j + 1 : 2 * j + 2, :] = jnp.sum(wide * wide, axis=0, keepdims=True)
                if depth < DEPTH:
                    wide = jnp.concatenate([wide, jnp.zeros((DEPTH - depth, width), jnp.float32)], axis=0)
                at = pl.ds(pl.multiple_of(k * width, width), width)
                if side == 0:
                    lhs[at, j * DEPTH : (j + 1) * DEPTH] = wide.T.astype(jnp.bfloat16)
                else:
                    rhs[j * DEPTH : (j + 1) * DEPTH, at] = wide.astype(jnp.bfloat16)
                return carry

            lax.fori_loop(0, C, piece, 0)

    def emit(b):
        def pair(side, k):
            mean_a, var_a = stats[side, k, 2 * b : 2 * b + 1, :], stats[side, k, 2 * b + 1 : 2 * b + 2, :]
            mean_b, var_b = stats[side, k, 2 * b + 2 : 2 * b + 3, :], stats[side, k, 2 * b + 3 : 2 * b + 4, :]
            delta = mean_a - mean_b
            return weight, delta, lax.rsqrt(var_a + var_b + weight * delta * delta)

        count_a = jnp.full((1, width), count(b).astype(jnp.float32))
        count_b = jnp.full((1, width), count(b + 1).astype(jnp.float32))
        weight = count_a * count_b / (count_a + count_b)
        cols = [pair(1, k)[1:] for k in range(C)]

        def tile(k, carry):
            w, delta, inv = pair(0, k)
            both = jnp.concatenate([w * delta, inv, jnp.zeros((6, width), jnp.float32)], axis=0).T
            scaled, inv_i = both[:, 0:1], both[:, 1:2]
            at = pl.ds(pl.multiple_of(k * width, width), width)
            a = lhs[at, b * DEPTH : (b + 2) * DEPTH]
            for m in range(C):
                span = slice(m * width, (m + 1) * width)
                gram = jnp.dot(a, rhs[b * DEPTH : (b + 2) * DEPTH, span], preferred_element_type=jnp.float32)
                cov = gram + scaled * cols[m][0]
                out_ref[b, at, span] = (cov * inv_i * cols[m][1]).astype(jnp.bfloat16)
            return carry

        lax.fori_loop(0, C, tile, 0)

    order = [last] + list(range(last))
    true = t >= 0
    mine = pltpu.make_async_copy(x_ref, raw.at[0, c, pl.ds(0, nbars)], own_sem)
    own_send(order[0])
    spread(true, order[0], c, x_ref.at[rows(order[0])])
    own_send(order[1])
    spread(true, order[1], c, x_ref.at[rows(order[1])])
    mine.start()

    @pl.when(t == 0)
    def _():
        low, depth = spans[before]
        for side in range(2):
            for k in range(C):
                raw[side, k, pl.ds(low, depth), :] = jnp.zeros((depth, width), jnp.bfloat16)

    for i, ch in enumerate(order):
        row_phase(ch)
        if i + 2 < nb:
            own_send(order[i + 2])
            spread(true, order[i + 2], c, x_ref.at[rows(order[i + 2])])
        if i >= 1:
            col_phase(order[i - 1], true)
        if i == 0:
            mine.wait()
        if i == 2:
            before_phase()
            center(last + 1)
            center(1)
        if i == nb - 1:
            col_phase(before, t > 0)
            center(0)
            emit(0)
            center(2)
            emit(1)
    col_phase(order[-1], true)
    for b in range(2, last):
        center(b + 1)
    for b in range(2, nb):
        emit(b)
    for there, make in sent:

        @pl.when(there)
        def _():
            make().wait_send()


def on_device(sizes, returns, block_bars):
    T, R, C = sizes
    nbars, width = returns.shape
    nb = block_bars.shape[0] // T
    blk = nbars // nb
    tail = nbars - down(blk * (nb - 1))
    dma = pltpu.SemaphoreType.DMA
    return pl.pallas_call(
        functools.partial(kernel, sizes, nb, blk),
        out_shape=jax.ShapeDtypeStruct((nb, C * width, R * width), jnp.bfloat16),
        in_specs=[pl.BlockSpec(memory_space=pltpu.SMEM), pl.BlockSpec(memory_space=pl.ANY)],
        out_specs=pl.BlockSpec(memory_space=pltpu.VMEM),
        scratch_shapes=[
            pltpu.VMEM((2, C, nbars + tail, width), jnp.bfloat16),
            pltpu.VMEM((C * width, (nb + 1) * DEPTH), jnp.bfloat16),
            pltpu.VMEM(((nb + 1) * DEPTH, R * width), jnp.bfloat16),
            pltpu.VMEM((2, C, up(2 * (nb + 1)), width), jnp.float32),
            dma,
            dma((nb, C, 2)),
            dma((nb + 1, C)),
            dma((C,)),
            dma((nb + 1, C, R // 2)),
            dma((nb + 1, C)),
            dma((nb + 1, C)),
        ],
        compiler_params=pltpu.CompilerParams(
            collective_id=0, has_side_effects=True, vmem_limit_bytes=48 * 1024 * 1024
        ),
        name="gather_correlate",
    )(block_bars, returns)


def solution(mesh):
    sizes = (mesh.shape["tm"], mesh.shape["row"], mesh.shape["col"])
    placed = (P("tm", ("row", "col")), P())
    return jax.shard_map(
        functools.partial(on_device, sizes),
        mesh=mesh, in_specs=placed, out_specs=P("tm", "row", "col"), check_vma=False,
    )
```

```python
import functools

import jax
import jax.numpy as jnp
from jax import lax
from jax.experimental import pallas as pl
from jax.experimental.pallas import tpu as pltpu
from jax.sharding import PartitionSpec as P

TILE = 16
DEPTH = 256
MESH = pl.DeviceIdType.MESH


def up(value, step=TILE):
    return -(-value // step) * step


def down(value, step=TILE):
    return value // step * step


def kernel(
    sizes, nb, blk, bars_ref, x_ref, out_ref,
    raw, lhs, rhs, stats, own_sem, row_send, row_recv, next_send, hub_send, col_recv, relay_send,
):
    T, R, C = sizes
    nbars, width = x_ref.shape
    t, r, c = lax.axis_index("tm"), lax.axis_index("row"), lax.axis_index("col")
    hub = r == c
    last = nb - 1
    cuts = [up(blk * b) for b in range(nb - 1)] + [down(blk * last), nbars]
    spans = [(cuts[b], cuts[b + 1] - cuts[b]) for b in range(nb)]
    spans.append((nbars, nbars - cuts[last]))
    before = nb

    def rows(ch):
        return pl.ds(*spans[ch])

    barrier = pltpu.get_barrier_semaphore()

    def greet(where):
        pl.semaphore_signal(barrier, inc=1, device_id=where, device_id_type=MESH)

    ends = ((c > 0, {"col": c - 1}), (c < C - 1, {"col": c + 1}), (t > 0, {"tm": t - 1}), (t < T - 1, {"tm": t + 1}))
    expected = R - 1
    for there, where in ends:
        pl.when(there)(functools.partial(greet, where))
        expected = expected + there.astype(jnp.int32)
    for step in range(1, R):
        greet({"row": lax.rem(r + step, R)})
    pl.semaphore_wait(barrier, expected)

    def remote(src, dst, send, recv, where):
        return pltpu.make_async_remote_copy(
            src_ref=src, dst_ref=dst, send_sem=send, recv_sem=recv, device_id=where, device_id_type=MESH
        )

    sent = []

    def start(there, make):
        @pl.when(there)
        def _():
            make().start()

        sent.append((there, make))

    def row_copy(ch, k, to_right, src):
        where = {"col": c + 1 if to_right else c - 1}
        return remote(src, raw.at[0, k, rows(ch)], row_send.at[ch, k, int(to_right)], row_recv.at[ch, k], where)

    def own_send(ch):
        src = x_ref.at[rows(ch)]
        start(c < C - 1, lambda: row_copy(ch, c, True, src))
        start(c > 0, lambda: row_copy(ch, c, False, src))

    def spread(there, ch, k, src):
        at_hub = jnp.logical_and(there, hub)
        chips = R // 2
        chip = r // 2
        for step in range(1, chips):
            where = {"row": 2 * lax.rem(chip + step, chips) + lax.rem(k, 2)}
            start(at_hub, lambda where=where, step=step: remote(
                src, raw.at[1, k, rows(ch)], hub_send.at[ch, k, step], col_recv.at[ch, k], where))
        partner = {"row": r + 1 - 2 * lax.rem(r, 2)}
        start(at_hub, lambda: remote(src, raw.at[1, k, rows(ch)], hub_send.at[ch, k, 0], col_recv.at[ch, k], partner))
        if ch == last:
            start(jnp.logical_and(there, t < T - 1), lambda: remote(
                src, raw.at[0, k, rows(before)], next_send.at[k], row_recv.at[before, k], {"tm": t + 1}))

    def row_arrive(there, ch, k):
        @pl.when(there)
        def _():
            piece = raw.at[0, k, rows(ch)]
            remote(piece, piece, next_send.at[k], row_recv.at[ch, k], {"row": r}).wait_recv()

    def row_phase(ch):
        for d in range(1, C):
            for from_left in (True, False):
                k0 = c - d if from_left else c + d
                there = k0 >= 0 if from_left else k0 < C
                k = jnp.clip(k0, 0, C - 1)
                row_arrive(there, ch, k)
                src = raw.at[0, k, rows(ch)]
                on = c < C - 1 if from_left else c > 0
                start(jnp.logical_and(there, on), lambda k=k, src=src, right=from_left: row_copy(ch, k, right, src))
                spread(there, ch, k, src)

    def before_phase():
        for k in range(C):
            row_arrive(t > 0, before, k)
            spread(t > 0, before, jnp.int32(k), raw.at[0, k, rows(before)])

    def col_phase(ch, there):
        relay = jnp.logical_and(there, r // 2 != c // 2)
        partner = {"row": r + 1 - 2 * lax.rem(r, 2)}
        for k in range(C):
            piece = raw.at[1, k, rows(ch)]

            @pl.when(jnp.logical_and(there, jnp.logical_not(hub)))
            def _():
                remote(piece, piece, next_send.at[k], col_recv.at[ch, k], {"row": r}).wait_recv()

            start(jnp.logical_and(relay, lax.rem(r, 2) == k % 2), lambda piece=piece, k=k: remote(
                piece, piece, relay_send.at[ch, k], col_recv.at[ch, k], partner))

    base = t * nb

    def count(j):
        if j:
            return bars_ref[base + j - 1]
        return jnp.where(t > 0, bars_ref[jnp.maximum(base - 1, 0)], 0)

    def center(j):
        b = j - 1 if j else last
        low = down(blk * b)
        depth = up(blk * (b + 1)) - low
        offset = blk * b - low
        first = low if j else spans[before][0]
        n = count(j)
        bar = lax.broadcasted_iota(jnp.int32, (depth, width), 0) - offset
        mask = jnp.logical_and(bar >= 0, bar < n)
        divisor = jnp.full((1, width), jnp.maximum(n, 1).astype(jnp.float32))
        for side in range(2):
            source = 0 if side == 0 else jnp.where(hub, 0, 1)

            def piece(k, carry):
                values = raw[source, k, pl.ds(first, depth), :].astype(jnp.float32)
                mean = jnp.sum(jnp.where(mask, values, 0.0), axis=0, keepdims=True) / divisor
                cent = jnp.where(mask, values - mean, 0.0).astype(jnp.bfloat16)
                wide = cent.astype(jnp.float32)
                stats[side, k, 2 * j : 2 * j + 1, :] = mean
                stats[side, k, 2 * j + 1 : 2 * j + 2, :] = jnp.sum(wide * wide, axis=0, keepdims=True)
                if depth < DEPTH:
                    wide = jnp.concatenate([wide, jnp.zeros((DEPTH - depth, width), jnp.float32)], axis=0)
                at = pl.ds(pl.multiple_of(k * width, width), width)
                if side == 0:
                    lhs[at, j * DEPTH : (j + 1) * DEPTH] = wide.T.astype(jnp.bfloat16)
                else:
                    rhs[j * DEPTH : (j + 1) * DEPTH, at] = wide.astype(jnp.bfloat16)
                return carry

            lax.fori_loop(0, C, piece, 0)

    def emit(b):
        def pair(side, k):
            mean_a, var_a = stats[side, k, 2 * b : 2 * b + 1, :], stats[side, k, 2 * b + 1 : 2 * b + 2, :]
            mean_b, var_b = stats[side, k, 2 * b + 2 : 2 * b + 3, :], stats[side, k, 2 * b + 3 : 2 * b + 4, :]
            delta = mean_a - mean_b
            return weight, delta, lax.rsqrt(var_a + var_b + weight * delta * delta)

        count_a = jnp.full((1, width), count(b).astype(jnp.float32))
        count_b = jnp.full((1, width), count(b + 1).astype(jnp.float32))
        weight = count_a * count_b / (count_a + count_b)
        cols = [pair(1, k)[1:] for k in range(C)]

        def tile(k, carry):
            w, delta, inv = pair(0, k)
            both = jnp.concatenate([w * delta, inv, jnp.zeros((6, width), jnp.float32)], axis=0).T
            scaled, inv_i = both[:, 0:1], both[:, 1:2]
            at = pl.ds(pl.multiple_of(k * width, width), width)
            a = lhs[at, b * DEPTH : (b + 2) * DEPTH]
            for m in range(C):
                span = slice(m * width, (m + 1) * width)
                gram = jnp.dot(a, rhs[b * DEPTH : (b + 2) * DEPTH, span], preferred_element_type=jnp.float32)
                cov = gram + scaled * cols[m][0]
                out_ref[b, at, span] = (cov * inv_i * cols[m][1]).astype(jnp.bfloat16)
            return carry

        lax.fori_loop(0, C, tile, 0)

    order = [last] + list(range(last))
    true = t >= 0
    mine = pltpu.make_async_copy(x_ref, raw.at[0, c, pl.ds(0, nbars)], own_sem)
    own_send(order[0])
    spread(true, order[0], c, x_ref.at[rows(order[0])])
    own_send(order[1])
    spread(true, order[1], c, x_ref.at[rows(order[1])])
    mine.start()

    @pl.when(t == 0)
    def _():
        low, depth = spans[before]
        for side in range(2):
            for k in range(C):
                raw[side, k, pl.ds(low, depth), :] = jnp.zeros((depth, width), jnp.bfloat16)

    for i, ch in enumerate(order):
        row_phase(ch)
        if i + 2 < nb:
            own_send(order[i + 2])
            spread(true, order[i + 2], c, x_ref.at[rows(order[i + 2])])
        if i >= 1:
            col_phase(order[i - 1], true)
        if i == 0:
            mine.wait()
        if i == 2:
            before_phase()
            center(last + 1)
            center(1)
        if i == nb - 1:
            col_phase(before, t > 0)
            center(0)
            emit(0)
            center(2)
            emit(1)
    col_phase(order[-1], true)
    for b in range(2, last):
        center(b + 1)
    for b in range(2, nb):
        emit(b)
    for there, make in sent:

        @pl.when(there)
        def _():
            make().wait_send()


def on_device(sizes, returns, block_bars):
    T, R, C = sizes
    nbars, width = returns.shape
    nb = block_bars.shape[0] // T
    blk = nbars // nb
    tail = nbars - down(blk * (nb - 1))
    dma = pltpu.SemaphoreType.DMA
    return pl.pallas_call(
        functools.partial(kernel, sizes, nb, blk),
        out_shape=pltpu.VMEM((nb, C * width, R * width), jnp.bfloat16),
        in_specs=[pl.BlockSpec(memory_space=pltpu.SMEM), pl.BlockSpec(memory_space=pl.ANY)],
        out_specs=pl.BlockSpec(memory_space=pltpu.VMEM),
        scratch_shapes=[
            pltpu.VMEM((2, C, nbars + tail, width), jnp.bfloat16),
            pltpu.VMEM((C * width, (nb + 1) * DEPTH), jnp.bfloat16),
            pltpu.VMEM(((nb + 1) * DEPTH, R * width), jnp.bfloat16),
            pltpu.VMEM((2, C, up(2 * (nb + 1)), width), jnp.float32),
            dma,
            dma((nb, C, 2)),
            dma((nb + 1, C)),
            dma((C,)),
            dma((nb + 1, C, R // 2)),
            dma((nb + 1, C)),
            dma((nb + 1, C)),
        ],
        compiler_params=pltpu.CompilerParams(
            collective_id=0, has_side_effects=True, vmem_limit_bytes=32 * 1024 * 1024
        ),
        name="gather_correlate",
    )(block_bars, returns)


def solution(mesh):
    sizes = (mesh.shape["tm"], mesh.shape["row"], mesh.shape["col"])
    placed = (P("tm", ("row", "col")), P())
    return jax.shard_map(
        functools.partial(on_device, sizes),
        mesh=mesh, in_specs=placed, out_specs=P("tm", "row", "col"), check_vma=False,
    )
```

```python
import functools

import jax
import jax.numpy as jnp
from jax import lax
from jax.experimental import pallas as pl
from jax.experimental.pallas import tpu as pltpu
from jax.sharding import PartitionSpec as P

TILE = 16
DEPTH = 256
LAG = 4
MESH = pl.DeviceIdType.MESH


def up(value, step=TILE):
    return -(-value // step) * step


def down(value, step=TILE):
    return value // step * step


def kernel(
    sizes, nb, blk, bars_in, x_ref, out_ref,
    bars_ref, raw, lhs, rhs, stats, kept, final, own_sem, bars_sem, row_send, row_recv, next_send, hub_send, col_recv, relay_send,
):
    T, R, C = sizes
    nbars, width = x_ref.shape
    t, r, c = lax.axis_index("tm"), lax.axis_index("row"), lax.axis_index("col")
    hub = r == c
    last = nb - 1
    cuts = [up(blk * b) for b in range(nb - 1)] + [down(blk * last), nbars]
    spans = [(cuts[b], cuts[b + 1] - cuts[b]) for b in range(nb)]
    spans.append((nbars, nbars - cuts[last]))
    before = nb

    def rows(ch):
        return pl.ds(*spans[ch])

    barrier = pltpu.get_barrier_semaphore()

    def greet(where):
        pl.semaphore_signal(barrier, inc=1, device_id=where, device_id_type=MESH)

    ends = ((c > 0, {"col": c - 1}), (c < C - 1, {"col": c + 1}), (t > 0, {"tm": t - 1}), (t < T - 1, {"tm": t + 1}))
    expected = R - 1
    for there, where in ends:
        pl.when(there)(functools.partial(greet, where))
        expected = expected + there.astype(jnp.int32)
    for step in range(1, R):
        greet({"row": lax.rem(r + step, R)})
    pl.semaphore_wait(barrier, expected)

    def remote(src, dst, send, recv, where):
        return pltpu.make_async_remote_copy(
            src_ref=src, dst_ref=dst, send_sem=send, recv_sem=recv, device_id=where, device_id_type=MESH
        )

    sent = []

    def start(there, make):
        @pl.when(there)
        def _():
            make().start()

        sent.append((there, make))

    def row_copy(ch, k, to_right, src):
        where = {"col": c + 1 if to_right else c - 1}
        return remote(src, raw.at[0, k, rows(ch)], row_send.at[ch, k, int(to_right)], row_recv.at[ch, k], where)

    def own_send(ch):
        src = x_ref.at[rows(ch)]
        start(c < C - 1, lambda: row_copy(ch, c, True, src))
        start(c > 0, lambda: row_copy(ch, c, False, src))

    def spread(there, ch, k, src):
        at_hub = jnp.logical_and(there, hub)
        chips = R // 2
        chip = r // 2
        for step in range(1, chips):
            where = {"row": 2 * lax.rem(chip + step, chips) + lax.rem(k, 2)}
            start(at_hub, lambda where=where, step=step: remote(
                src, raw.at[1, k, rows(ch)], hub_send.at[ch, k, step], col_recv.at[ch, k], where))
        partner = {"row": r + 1 - 2 * lax.rem(r, 2)}
        start(at_hub, lambda: remote(src, raw.at[1, k, rows(ch)], hub_send.at[ch, k, 0], col_recv.at[ch, k], partner))
        if ch == last:
            start(jnp.logical_and(there, t < T - 1), lambda: remote(
                src, raw.at[0, k, rows(before)], next_send.at[k], row_recv.at[before, k], {"tm": t + 1}))

    def row_arrive(there, ch, k):
        @pl.when(there)
        def _():
            piece = raw.at[0, k, rows(ch)]
            remote(piece, piece, next_send.at[k], row_recv.at[ch, k], {"row": r}).wait_recv()

    def row_event(ch, k, there, on, to_right):
        if to_right is None and ch != before:
            return
        row_arrive(there, ch, k)
        src = raw.at[0, k, rows(ch)]
        if ch != before:
            start(jnp.logical_and(there, on), lambda: row_copy(ch, k, to_right, src))
        spread(there, ch, k, src)

    def col_event(ch, k, there):
        relay = jnp.logical_and(there, r // 2 != c // 2)
        partner = {"row": r + 1 - 2 * lax.rem(r, 2)}
        piece = raw.at[1, k, rows(ch)]

        @pl.when(jnp.logical_and(there, jnp.logical_not(hub)))
        def _():
            remote(piece, piece, next_send.at[k], col_recv.at[ch, k], {"row": r}).wait_recv()

        start(jnp.logical_and(relay, lax.rem(r, 2) == lax.rem(k, 2)), lambda: remote(
            piece, piece, relay_send.at[ch, k], col_recv.at[ch, k], partner))

    base = t * nb

    def count(j):
        if j:
            return bars_ref[base + j - 1]
        return jnp.where(t > 0, bars_ref[jnp.maximum(base - 1, 0)], 0)

    def center(j, side):
        b = j - 1 if j else last
        low = down(blk * b)
        depth = up(blk * (b + 1)) - low
        offset = blk * b - low
        first = low if j else spans[before][0]
        n = count(j)
        bar = lax.broadcasted_iota(jnp.int32, (depth, width), 0) - offset
        mask = jnp.logical_and(bar >= 0, bar < n)
        divisor = jnp.full((1, width), jnp.maximum(n, 1).astype(jnp.float32))
        source = 0 if side == 0 else jnp.where(hub, 0, 1)

        def piece(k, carry):
            values = raw[source, k, pl.ds(first, depth), :].astype(jnp.float32)
            mean = jnp.sum(jnp.where(mask, values, 0.0), axis=0, keepdims=True) / divisor
            cent = jnp.where(mask, values - mean, 0.0).astype(jnp.bfloat16)
            wide = cent.astype(jnp.float32)
            stats[side, k, 2 * j : 2 * j + 1, :] = mean
            stats[side, k, 2 * j + 1 : 2 * j + 2, :] = jnp.sum(wide * wide, axis=0, keepdims=True)
            if depth < DEPTH:
                wide = jnp.concatenate([wide, jnp.zeros((DEPTH - depth, width), jnp.float32)], axis=0)
            at = pl.ds(pl.multiple_of(k * width, width), width)
            if side == 0:
                lhs[at, j * DEPTH : (j + 1) * DEPTH] = wide.T.astype(jnp.bfloat16)
            else:
                rhs[j * DEPTH : (j + 1) * DEPTH, at] = wide.astype(jnp.bfloat16)
            return carry

        lax.fori_loop(0, C, piece, 0)

    def weigh(b):
        count_a = jnp.full((1, width), count(b).astype(jnp.float32))
        count_b = jnp.full((1, width), count(b + 1).astype(jnp.float32))
        return count_a * count_b / (count_a + count_b)

    def pair(b, weight, side, k):
        mean_a, var_a = stats[side, k, 2 * b : 2 * b + 1, :], stats[side, k, 2 * b + 1 : 2 * b + 2, :]
        mean_b, var_b = stats[side, k, 2 * b + 2 : 2 * b + 3, :], stats[side, k, 2 * b + 3 : 2 * b + 4, :]
        delta = mean_a - mean_b
        return delta, lax.rsqrt(var_a + var_b + weight * delta * delta)

    def gram_tile(k, j, uses, keep):
        at = slice(k * width, (k + 1) * width)
        sides = []
        for b, other in uses:
            weight = weigh(b)
            delta, inv = pair(b, weight, 0, k)
            both = jnp.concatenate([weight * delta, inv, jnp.zeros((6, width), jnp.float32)], axis=0).T
            sides.append((b, other, weight, both[:, 0:1], both[:, 1:2]))
        a = lhs[at, j * DEPTH : (j + 1) * DEPTH]
        for m in range(R):
            span = slice(m * width, (m + 1) * width)
            gram = jnp.dot(a, rhs[j * DEPTH : (j + 1) * DEPTH, span], preferred_element_type=jnp.float32)
            for b, other, weight, scaled, inv_i in sides:
                delta, inv = pair(b, weight, 1, m)
                cov = gram + other[at, span] + scaled * delta
                out_ref[b, at, span] = (cov * inv_i * inv).astype(jnp.bfloat16)
            if keep is not None:
                keep[at, span] = gram

    order = [last] + list(range(last))
    true = t >= 0
    mine = pltpu.make_async_copy(x_ref, raw.at[0, c, pl.ds(0, nbars)], own_sem)
    bars_copy = pltpu.make_async_copy(bars_in, bars_ref, bars_sem)
    for ch in order[:2]:
        own_send(ch)
        spread(true, ch, c, x_ref.at[rows(ch)])
    mine.start()
    bars_copy.start()

    @pl.when(t == 0)
    def _():
        low, depth = spans[before]
        for side in range(2):
            for k in range(C):
                raw[side, k, pl.ds(low, depth), :] = jnp.zeros((depth, width), jnp.bfloat16)

    events = []
    for i, ch in enumerate(order):
        events.append((ch, c, true, true, None))
        for d in range(1, C):
            events.append((ch, jnp.maximum(c - d, 0), c >= d, c < C - 1, True))
            events.append((ch, jnp.minimum(c + d, C - 1), c + d < C, c > 0, False))
        if i == 1:
            events.extend((before, jnp.int32(k), t > 0, true, None) for k in range(C))

    def ready(j):
        if j == 0:
            needed = {before}
        else:
            low, high = down(blk * (j - 1)), up(blk * j)
            needed = {ch for ch in range(nb) if cuts[ch] < high and cuts[ch + 1] > low}
        return max(e for e, event in enumerate(events) if event[0] in needed)

    tasks = []

    def plan(j, uses, keep):
        for side in range(2):
            tasks.append((ready(j), functools.partial(center, j, side)))
        for k in range(C):
            tasks.append((ready(j), functools.partial(gram_tile, k, j, uses, keep)))

    plan(nb, [], final)
    plan(1, [], kept)
    plan(0, [(0, kept)], None)
    for b in range(1, last):
        uses = [(b, kept)] + ([(last, final)] if b == last - 1 else [])
        plan(b + 1, uses, kept if b < last - 1 else None)

    waited = False
    for e in range(len(events) + LAG):
        if e < len(events):
            row_event(*events[e])
            if e + 1 == len(events) or (events[e + 1][0] != events[e][0]):
                if events[e][0] != before and order.index(events[e][0]) + 2 < nb:
                    ch = order[order.index(events[e][0]) + 2]
                    own_send(ch)
                    spread(true, ch, c, x_ref.at[rows(ch)])
        if e >= LAG:
            col_event(*events[e - LAG][:3])
        if tasks and tasks[0][0] <= e - LAG:
            if not waited:
                mine.wait()
                bars_copy.wait()
                waited = True
            tasks.pop(0)[1]()
    for _, task in tasks:
        task()
    for there, make in sent:

        @pl.when(there)
        def _():
            make().wait_send()


def on_device(sizes, returns, block_bars):
    T, R, C = sizes
    nbars, width = returns.shape
    nb = block_bars.shape[0] // T
    blk = nbars // nb
    tail = nbars - down(blk * (nb - 1))
    dma = pltpu.SemaphoreType.DMA
    return pl.pallas_call(
        functools.partial(kernel, sizes, nb, blk),
        out_shape=pltpu.VMEM((nb, C * width, R * width), jnp.bfloat16),
        in_specs=[pl.BlockSpec(memory_space=pltpu.HBM), pl.BlockSpec(memory_space=pltpu.HBM)],
        out_specs=pl.BlockSpec(memory_space=pltpu.VMEM),
        scratch_shapes=[
            pltpu.SMEM(block_bars.shape, jnp.int32),
            pltpu.VMEM((2, C, nbars + tail, width), jnp.bfloat16),
            pltpu.VMEM((C * width, (nb + 1) * DEPTH), jnp.bfloat16),
            pltpu.VMEM(((nb + 1) * DEPTH, R * width), jnp.bfloat16),
            pltpu.VMEM((2, C, up(2 * (nb + 1)), width), jnp.float32),
            pltpu.VMEM((C * width, R * width), jnp.float32),
            pltpu.VMEM((C * width, R * width), jnp.float32),
            dma,
            dma,
            dma((nb, C, 2)),
            dma((nb + 1, C)),
            dma((C,)),
            dma((nb + 1, C, R // 2)),
            dma((nb + 1, C)),
            dma((nb + 1, C)),
        ],
        compiler_params=pltpu.CompilerParams(
            collective_id=0, has_side_effects=True, vmem_limit_bytes=32 * 1024 * 1024
        ),
        name="gather_correlate",
    )(block_bars, returns)


def solution(mesh):
    sizes = (mesh.shape["tm"], mesh.shape["row"], mesh.shape["col"])
    placed = (P("tm", ("row", "col")), P())
    return jax.shard_map(
        functools.partial(on_device, sizes),
        mesh=mesh, in_specs=placed, out_specs=P("tm", "row", "col"), check_vma=False,
    )
```

```python
import functools

import jax
import jax.numpy as jnp
from jax import lax
from jax.experimental import pallas as pl
from jax.experimental.pallas import tpu as pltpu
from jax.sharding import PartitionSpec as P

TILE = 16
DEPTH = 256
MESH = pl.DeviceIdType.MESH


def up(value, step=TILE):
    return -(-value // step) * step


def down(value, step=TILE):
    return value // step * step


def kernel(
    sizes, nb, blk, bars_in, x_ref, out_ref,
    bars_ref, raw, lhs, rhs, row_stats, col_stats, own_sem, bars_sem, row_send, row_recv, next_send, hub_send, col_recv, relay_send,
):
    T, R, C = sizes
    nbars, width = x_ref.shape
    t, r, c = lax.axis_index("tm"), lax.axis_index("row"), lax.axis_index("col")
    hub = r == c
    last = nb - 1
    cuts = [up(blk * b) for b in range(nb - 1)] + [down(blk * last), nbars]
    spans = [(cuts[b], cuts[b + 1] - cuts[b]) for b in range(nb)]
    spans.append((nbars, nbars - cuts[last]))
    before = nb

    def rows(ch):
        return pl.ds(*spans[ch])

    barrier = pltpu.get_barrier_semaphore()

    def greet(where):
        pl.semaphore_signal(barrier, inc=1, device_id=where, device_id_type=MESH)

    ends = ((c > 0, {"col": c - 1}), (c < C - 1, {"col": c + 1}), (t > 0, {"tm": t - 1}), (t < T - 1, {"tm": t + 1}))
    expected = R - 1
    for there, where in ends:
        pl.when(there)(functools.partial(greet, where))
        expected = expected + there.astype(jnp.int32)
    for step in range(1, R):
        greet({"row": lax.rem(r + step, R)})
    pl.semaphore_wait(barrier, expected)

    def remote(src, dst, send, recv, where):
        return pltpu.make_async_remote_copy(
            src_ref=src, dst_ref=dst, send_sem=send, recv_sem=recv, device_id=where, device_id_type=MESH
        )

    sent = []

    def start(there, make):
        @pl.when(there)
        def _():
            make().start()

        sent.append((there, make))

    def row_copy(ch, k, to_right, src):
        where = {"col": c + 1 if to_right else c - 1}
        return remote(src, raw.at[0, k, rows(ch)], row_send.at[ch, k, int(to_right)], row_recv.at[ch, k], where)

    def own_send(ch):
        src = x_ref.at[rows(ch)]
        start(c < C - 1, lambda: row_copy(ch, c, True, src))
        start(c > 0, lambda: row_copy(ch, c, False, src))

    def spread(there, ch, k, src):
        at_hub = jnp.logical_and(there, hub)
        chips = R // 2
        chip = r // 2
        for step in range(1, chips):
            where = {"row": 2 * lax.rem(chip + step, chips) + lax.rem(k, 2)}
            start(at_hub, lambda where=where, step=step: remote(
                src, raw.at[1, k, rows(ch)], hub_send.at[ch, k, step], col_recv.at[ch, k], where))
        partner = {"row": r + 1 - 2 * lax.rem(r, 2)}
        start(at_hub, lambda: remote(src, raw.at[1, k, rows(ch)], hub_send.at[ch, k, 0], col_recv.at[ch, k], partner))
        if ch == last:
            start(jnp.logical_and(there, t < T - 1), lambda: remote(
                src, raw.at[0, k, rows(before)], next_send.at[k], row_recv.at[before, k], {"tm": t + 1}))

    def row_arrive(there, ch, k):
        @pl.when(there)
        def _():
            piece = raw.at[0, k, rows(ch)]
            remote(piece, piece, next_send.at[k], row_recv.at[ch, k], {"row": r}).wait_recv()

    def row_event(ch, k, there, on, to_right):
        if to_right is None and ch != before:
            return
        row_arrive(there, ch, k)
        src = raw.at[0, k, rows(ch)]
        if ch != before:
            start(jnp.logical_and(there, on), lambda: row_copy(ch, k, to_right, src))
        spread(there, ch, k, src)

    def col_event(ch, k, there):
        relay = jnp.logical_and(there, r // 2 != c // 2)
        partner = {"row": r + 1 - 2 * lax.rem(r, 2)}
        piece = raw.at[1, k, rows(ch)]

        @pl.when(jnp.logical_and(there, jnp.logical_not(hub)))
        def _():
            remote(piece, piece, next_send.at[k], col_recv.at[ch, k], {"row": r}).wait_recv()

        start(jnp.logical_and(relay, lax.rem(r, 2) == lax.rem(k, 2)), lambda: remote(
            piece, piece, relay_send.at[ch, k], col_recv.at[ch, k], partner))

    base = t * nb

    def count(j):
        if j:
            return bars_ref[base + j - 1]
        return jnp.where(t > 0, bars_ref[jnp.maximum(base - 1, 0)], 0)

    def moments(j, n, values):
        b = j - 1 if j else last
        low = down(blk * b)
        depth = up(blk * (b + 1)) - low
        offset = blk * b - low
        first = low if j else spans[before][0]
        bar = lax.broadcasted_iota(jnp.int32, (depth, width), 0) - offset
        mask = jnp.logical_and(bar >= 0, bar < n)
        values = values(first, depth).astype(jnp.float32)
        divisor = jnp.full((1, width), jnp.maximum(n, 1).astype(jnp.float32))
        mean = jnp.sum(jnp.where(mask, values, 0.0), axis=0, keepdims=True) / divisor
        wide = jnp.where(mask, values - mean, 0.0).astype(jnp.bfloat16).astype(jnp.float32)
        var = jnp.sum(wide * wide, axis=0, keepdims=True)
        if depth < DEPTH:
            wide = jnp.concatenate([wide, jnp.zeros((DEPTH - depth, width), jnp.float32)], axis=0)
        return mean, var, wide

    def center(k):
        at = pl.ds(pl.multiple_of(k * width, width), width)
        counts = [count(j) for j in range(nb + 1)]
        for side in range(2):
            source = 0 if side == 0 else jnp.where(hub, 0, 1)
            means, variances = [], []
            for j in range(nb + 1):
                mean, var, wide = moments(j, counts[j], lambda first, depth: raw[source, k, pl.ds(first, depth), :])
                means.append(mean)
                variances.append(var)
                if side == 0:
                    lhs[at, j * DEPTH : (j + 1) * DEPTH] = wide.T.astype(jnp.bfloat16)
                else:
                    rhs[j * DEPTH : (j + 1) * DEPTH, at] = wide.astype(jnp.bfloat16)
            lines = []
            for b in range(nb):
                count_a = jnp.full((1, width), counts[b].astype(jnp.float32))
                count_b = jnp.full((1, width), counts[b + 1].astype(jnp.float32))
                weight = count_a * count_b / (count_a + count_b)
                delta = means[b] - means[b + 1]
                inv = lax.rsqrt(variances[b] + variances[b + 1] + weight * delta * delta)
                lines.extend([weight * delta if side == 0 else delta, inv])
            spare = up(2 * nb, 8) - 2 * nb
            if spare:
                lines.append(jnp.zeros((spare, width), jnp.float32))
            lines = jnp.concatenate(lines, axis=0)
            if side == 0:
                row_stats[k] = lines.T
            else:
                col_stats[k] = lines

    def tile(kr, kc):
        down_at = pl.ds(pl.multiple_of(kr * width, width), width)
        over_at = pl.ds(pl.multiple_of(kc * width, width), width)
        previous = None
        for j in range(nb + 1):
            span = slice(j * DEPTH, (j + 1) * DEPTH)
            gram = jnp.dot(lhs[down_at, span], rhs[span, over_at], preferred_element_type=jnp.float32)
            if j:
                b = j - 1
                scaled, inv_i = row_stats[kr, :, 2 * b : 2 * b + 1], row_stats[kr, :, 2 * b + 1 : 2 * b + 2]
                delta, inv = col_stats[kc, 2 * b : 2 * b + 1, :], col_stats[kc, 2 * b + 1 : 2 * b + 2, :]
                cov = previous + gram + scaled * delta
                out_ref[b, down_at, over_at] = (cov * inv_i * inv).astype(jnp.bfloat16)
            previous = gram

    near = jnp.minimum(c, C - 1 - c)

    def source_at(p):
        both = jnp.where(lax.rem(p, 2) == 1, c - (p + 1) // 2, c + p // 2)
        one = jnp.where(2 * c < C - 1, c + p - near, c - p + near)
        return jnp.where(p <= 2 * near, both, one)

    def within(d):
        return jnp.minimum(c, d) + jnp.minimum(C - 1 - c, d) + 1

    def compute(d):
        def shell(p, carry):
            k = source_at(p)
            center(k)

            def one(n, carry):
                other = source_at(jnp.where(n <= p, n, n - p - 1))
                tile(jnp.where(n <= p, k, other), jnp.where(n <= p, other, k))
                return carry

            return lax.fori_loop(0, 2 * p + 1, one, carry)

        lax.fori_loop(within(d - 1) if d else 0, within(d), shell, 0)

    order = [last] + list(range(last))
    true = t >= 0
    mine = pltpu.make_async_copy(x_ref, raw.at[0, c, pl.ds(0, nbars)], own_sem)
    bars_copy = pltpu.make_async_copy(bars_in, bars_ref, bars_sem)
    for ch in order:
        own_send(ch)
        spread(true, ch, c, x_ref.at[rows(ch)])
    mine.start()
    bars_copy.start()

    @pl.when(t == 0)
    def _():
        low, depth = spans[before]
        for side in range(2):
            for k in range(C):
                raw[side, k, pl.ds(low, depth), :] = jnp.zeros((depth, width), jnp.bfloat16)

    def at_distance(d):
        if d == 0:
            return [(c, true, True)]
        return [(jnp.maximum(c - d, 0), c >= d, True), (jnp.minimum(c + d, C - 1), c + d < C, False)]

    def row_events(ch, d):
        for k, there, to_right in at_distance(d):
            if ch == before:
                row_event(ch, k, jnp.logical_and(there, t > 0), true, None)
            else:
                row_event(ch, k, there, c < C - 1 if to_right else c > 0, to_right)

    def col_events(ch, d):
        for k, there, _ in at_distance(d):
            col_event(ch, k, jnp.logical_and(there, t > 0) if ch == before else there)

    for d in range(1, C + 1):
        for i, ch in enumerate(order):
            if d < C:
                row_events(ch, d)
            if i == 0:
                row_events(before, d - 1)
                for other in order:
                    col_events(other, d - 1)
            if i == 1:
                col_events(before, d - 1)
                if d == 1:
                    mine.wait()
                    bars_copy.wait()
                compute(d - 1)
    for there, make in sent:

        @pl.when(there)
        def _():
            make().wait_send()


def on_device(sizes, returns, block_bars):
    T, R, C = sizes
    nbars, width = returns.shape
    nb = block_bars.shape[0] // T
    blk = nbars // nb
    tail = nbars - down(blk * (nb - 1))
    dma = pltpu.SemaphoreType.DMA
    return pl.pallas_call(
        functools.partial(kernel, sizes, nb, blk),
        out_shape=pltpu.VMEM((nb, C * width, R * width), jnp.bfloat16),
        in_specs=[pl.BlockSpec(memory_space=pltpu.HBM), pl.BlockSpec(memory_space=pltpu.HBM)],
        out_specs=pl.BlockSpec(memory_space=pltpu.VMEM),
        scratch_shapes=[
            pltpu.SMEM(block_bars.shape, jnp.int32),
            pltpu.VMEM((2, C, nbars + tail, width), jnp.bfloat16),
            pltpu.VMEM((C * width, (nb + 1) * DEPTH), jnp.bfloat16),
            pltpu.VMEM(((nb + 1) * DEPTH, R * width), jnp.bfloat16),
            pltpu.VMEM((C, width, up(2 * nb, 8)), jnp.float32),
            pltpu.VMEM((C, up(2 * nb, 8), width), jnp.float32),
            dma,
            dma,
            dma((nb, C, 2)),
            dma((nb + 1, C)),
            dma((C,)),
            dma((nb + 1, C, R // 2)),
            dma((nb + 1, C)),
            dma((nb + 1, C)),
        ],
        compiler_params=pltpu.CompilerParams(
            collective_id=0, has_side_effects=True, vmem_limit_bytes=58650624
        ),
        name="gather_correlate",
    )(block_bars, returns)


def solution(mesh):
    sizes = (mesh.shape["tm"], mesh.shape["row"], mesh.shape["col"])
    placed = (P("tm", ("row", "col")), P())
    return jax.shard_map(
        functools.partial(on_device, sizes),
        mesh=mesh, in_specs=placed, out_specs=P("tm", "row", "col"), check_vma=False,
    )
```
